32 devices in a mesh: seq: 4 (over y, x), dp: 4 (over z), enc: 2 (over core).
Axes of the slice: x: 2, y: 2, z: 4, core: 2. Of those that a mesh axis runs over, the one named last changes fastest.
Arguments:
- lm_grad: bfloat16 [4, 4, 192, 1152], P('dp', 'enc', 'seq'), may hold values from -6 to 6
- image_tokens: int32 [4, 4, 4], P('dp'), may hold values from 1 to 15, as said below
- image_offset: int32 [4, 4, 4], P('dp'), may hold values from 0 to 47, as said below
- image_owner: int32 [4, 4, 4], P('dp'), may hold values from 0 to 3, as said below
- mlp_input: bfloat16 [4, 4, 240, 1152], P('dp', None, 'seq'), may hold values from -36 to 36
- layer_output: bfloat16 [4, 4, 240, 1152], P('dp', 'enc', 'seq'), may hold values from -36 to 36
- pre_gain: float32 [1152], replicated, may hold values from 0.5 to 1.5
- pre_bias: float32 [1152], replicated, may hold values from -3 to 3
- fc1_weight: bfloat16 [1152, 4304], P(None, 'enc'), may hold values from -0.1875 to 0.1875
- fc1_bias: float32 [4304], P('enc'), may hold values from -3 to 3
- fc2_weight: bfloat16 [4304, 1152], P('enc'), may hold values from -0.09375 to 0.09375
- post_gain: float32 [1152], replicated, may hold values from 0.5 to 1.5
- post_bias: float32 [1152], replicated, may hold values from -3 to 3
- merge_gain: float32 [1152], replicated, may hold values from 0.5 to 1.5
Outputs:
- act_grad: bfloat16 [4, 4, 240, 1152], P('dp', 'enc', 'seq')
- norm_grads: float32 [6, 1152], replicated
- fc1_bias_grad: float32 [4304], replicated
The draws below stay inside these ranges and needn't reach their ends.
Inputs may be any that keep to these rules, and one draw needn't show every extreme that they name: `image_tokens`: the 4 images of one LM shard have token counts that sum to 48, and one of them has 15. `image_offset`: the images of one LM shard lie back to back over its 48 rows, in some order; each entry is an image's first row in its shard. Images are placed round-robin by their index j in a shard: image_owner[r, q, j] = (q + image_owner[r, 0, j]) mod 4, with the 4 values image_owner[r, 0, j] different. So each encoder chip owns exactly 4 images of its replica, the visual tokens owned by one chip number at most 60, and some chip owns exactly 60.
All inputs are finite; a program needn't handle non-finite values.
Results may differ from the reference program's by a relative error of at most 0.005.
Values may be sent and summed in bfloat16 or wider, within the bound.
A program may use at most 64 MiB of HBM per device.

```python
import math
import jax
import jax.numpy as jnp
from jax import lax

D = 1152
FF = 4304
PATCH_GROUP = 4
IMG_SHARD = 4
MOST_LEN = 15
ROWS_DEV = 48
CAP_TOK = 60
SHARDS = 4
REPLICAS = 4
PATCHES = 3072


def other_lengths(key):
    others = IMG_SHARD - 1
    spare = ROWS_DEV - MOST_LEN - others
    room = MOST_LEN - 1
    keys = jax.random.split(key, others + 1)
    rank = jax.vmap(lambda k: jax.random.permutation(k, others))(jax.random.split(keys[0], SHARDS)).astype(jnp.int32)
    extras = (spare // others + (rank < spare % others).astype(jnp.int32)).astype(jnp.int32)
    if others >= 2:
        for turn in range(others):
            first = turn
            second = (turn + 1) % others
            lower = -jnp.minimum(extras[:, first], room - extras[:, second])
            upper = jnp.minimum(extras[:, second], room - extras[:, first])
            moved = jax.random.randint(keys[turn + 1], (SHARDS,), lower, upper + 1, dtype=jnp.int32)
            extras = extras.at[:, first].add(moved).at[:, second].add(-moved)
    return (1 + extras).astype(jnp.int32)


def replica_tables(key):
    keys = jax.random.split(key, 6)
    shard_ids = jnp.arange(SHARDS, dtype=jnp.int32)
    class_ids = jnp.arange(IMG_SHARD, dtype=jnp.int32)
    shifts = jax.random.permutation(keys[1], SHARDS).astype(jnp.int32)[:IMG_SHARD]
    heavy = jax.random.randint(keys[2], (), 0, SHARDS, dtype=jnp.int32)
    target = (shard_ids[:, None] + shifts[None, :]) % SHARDS
    owners = target
    forced = target == heavy
    is_forced = jnp.any(forced, axis=1)
    forced_class = jnp.sum(jnp.where(forced, class_ids[None, :], 0), axis=1)
    free_pick = jax.random.randint(keys[3], (SHARDS,), 0, IMG_SHARD, dtype=jnp.int32)
    big_class = jnp.where(is_forced, forced_class, free_pick)
    composed = other_lengths(keys[4])
    take_index = jnp.clip(class_ids[None, :] - (class_ids[None, :] > big_class[:, None]).astype(jnp.int32), 0, IMG_SHARD - 2)
    lengths = jnp.where(class_ids[None, :] == big_class[:, None], MOST_LEN, jnp.take_along_axis(composed, take_index, axis=1))
    order_keys = jax.random.randint(keys[5], (SHARDS, IMG_SHARD), 0, 1024, dtype=jnp.int32) * IMG_SHARD + class_ids[None, :]
    earlier = order_keys[:, :, None] < order_keys[:, None, :]
    offsets = jnp.sum(jnp.where(earlier, lengths[:, :, None], 0), axis=1)
    return (lengths.astype(jnp.int32), offsets.astype(jnp.int32), owners.astype(jnp.int32))


def all_tables(key):
    keys = jax.random.split(jax.random.fold_in(key, 7), REPLICAS)
    return jax.vmap(replica_tables)(keys)


def draw_image_tokens(key, part):
    return all_tables(key)[0]


def draw_image_offset(key, part):
    return all_tables(key)[1]


def draw_image_owner(key, part):
    return all_tables(key)[2]


def activation_rows(key):
    keys = jax.random.split(key, 3)
    shape = (REPLICAS, PATCH_GROUP, SHARDS * CAP_TOK, D)
    column_scale = jnp.exp(jax.random.uniform(keys[0], (D,), jnp.float32, math.log(0.3), math.log(3.0)))
    row_scale = jnp.exp(jax.random.uniform(keys[1], (REPLICAS, PATCH_GROUP, SHARDS * CAP_TOK, 1), jnp.float32, math.log(0.3), math.log(3.0)))
    base = jnp.clip(jax.random.normal(keys[2], shape, jnp.float32), -4.0, 4.0)
    return (base * row_scale * column_scale).astype(jnp.bfloat16)


def draw_mlp_input(key, part):
    return activation_rows(jax.random.fold_in(key, 11))


def draw_layer_output(key, part):
    return activation_rows(jax.random.fold_in(key, 23))


def steps_of(key, shape, cuts, low, high):
    def one(dim, shards_of):
        draws = jax.random.uniform(jax.random.fold_in(jax.random.fold_in(key, 6), dim), (shards_of,), jnp.float32, low / len(cuts), high / len(cuts))
        return jnp.repeat(jnp.exp(draws), shape[dim] // shards_of).reshape((-1,) + (1,) * (len(shape) - dim - 1))

    factor_of = one(*cuts[0])
    for cut in cuts[1:]:
        factor_of = factor_of * one(*cut)
    return factor_of


def bell_draw(own_key, dims, width, bound, pieces=(), held_as=jnp.bfloat16):
    array = jax.random.normal(own_key, dims, jnp.float32) * width
    if len(pieces) > 0:
        array = steps_of(own_key, dims, pieces, -0.22, 0.18) * array
    return jnp.clip(array, min=-bound, max=bound).astype(held_as)


def setup_inputs(seed: int = 0) -> dict:
    key_of = jax.random.split(jax.random.key(seed), 15)
    lm_grad = bell_draw(key_of[0], (REPLICAS, PATCH_GROUP, SHARDS * ROWS_DEV, D), 1.0, 6.0, ((0, 4), (1, 2), (2, 4)))
    image_tokens = draw_image_tokens(jax.random.fold_in(key_of[14], 71), 0)
    image_offset = draw_image_offset(jax.random.fold_in(key_of[14], 71), 0)
    image_owner = draw_image_owner(jax.random.fold_in(key_of[14], 71), 0)
    mlp_input = draw_mlp_input(jax.random.fold_in(key_of[14], 71), 0)
    layer_output = draw_layer_output(jax.random.fold_in(key_of[14], 71), 0)
    pre_gain = jnp.clip(1.0 + 0.1 * jax.random.normal(key_of[6], (D,), jnp.float32), 0.5, 1.5)
    pre_bias = bell_draw(key_of[7], (D,), 0.5, 3.0, (), jnp.float32)
    fc1_weight = bell_draw(key_of[8], (D, FF), D ** -0.5, 0.1875, ((1, 2),))
    fc1_bias = bell_draw(key_of[9], (FF,), 0.5, 3.0, ((0, 2),), jnp.float32)
    fc2_weight = bell_draw(key_of[10], (FF, D), FF ** -0.5, 0.09375, ((0, 2),))
    post_gain = jnp.clip(1.0 + 0.1 * jax.random.normal(key_of[11], (D,), jnp.float32), 0.5, 1.5)
    post_bias = bell_draw(key_of[12], (D,), 0.5, 3.0, (), jnp.float32)
    merge_gain = jnp.clip(1.0 + 0.1 * jax.random.normal(key_of[13], (D,), jnp.float32), 0.5, 1.5)
    return {"lm_grad": lm_grad, "image_tokens": image_tokens, "image_offset": image_offset, "image_owner": image_owner, "mlp_input": mlp_input, "layer_output": layer_output, "pre_gain": pre_gain, "pre_bias": pre_bias, "fc1_weight": fc1_weight, "fc1_bias": fc1_bias, "fc2_weight": fc2_weight, "post_gain": post_gain, "post_bias": post_bias, "merge_gain": merge_gain}


EPSILON = 1e-06
SLOPE_K = math.sqrt(2.0 / math.pi)
CUBIC = 0.044715

def layer_norm(values):
    row_mean = lax.optimization_barrier(jnp.mean(values, axis=-1, keepdims=True))
    centred = values - row_mean
    return centred * lax.rsqrt(lax.optimization_barrier(jnp.mean(centred * centred, axis=-1, keepdims=True)) + EPSILON)

def rms_norm(values):
    return values * lax.rsqrt(lax.optimization_barrier(jnp.mean(values * values, axis=-1, keepdims=True)) + EPSILON)

def gelu_slope(pre_act):
    inner_arg = SLOPE_K * (pre_act + CUBIC * pre_act * pre_act * pre_act)
    tangent = jnp.tanh(inner_arg)
    return 0.5 * (1.0 + tangent) + 0.5 * pre_act * (1.0 - tangent * tangent) * SLOPE_K * (1.0 + 3.0 * CUBIC * pre_act * pre_act)

def head_back(incoming, layer_rows, merge_gain, post_gain, post_bias):

    def merge_head(row_values, merge_scale, post_scale, post_shift):
        return rms_norm(layer_norm(row_values) * post_scale + post_shift) * merge_scale
    _, pullback = jax.vjp(merge_head, layer_rows.astype(jnp.float32), merge_gain, post_gain, post_bias)
    return pullback(incoming.astype(jnp.float32))

def pre_back(input_rows, pre_gain, pre_bias, upstream):

    def prenorm(row_values, scale_vec, shift_vec):
        return layer_norm(row_values) * scale_vec + shift_vec
    _, pullback = jax.vjp(prenorm, input_rows.astype(jnp.float32), pre_gain, pre_bias)
    return pullback(upstream)

def slot_source(lengths, offsets, owners, chip_index):
    shard_count = lengths.shape[0]
    is_mine = owners == chip_index
    my_len = lax.optimization_barrier(jnp.sum(jnp.where(is_mine, lengths, 0), axis=1)).astype(jnp.int32)
    my_off = lax.optimization_barrier(jnp.sum(jnp.where(is_mine, offsets, 0), axis=1)).astype(jnp.int32)
    slot_first = (jnp.cumsum(my_len) - my_len).astype(jnp.int32)
    slot_ids = jnp.arange(CAP_TOK, dtype=jnp.int32)
    inside = (slot_ids[:, None] >= slot_first[None, :]) & (slot_ids[:, None] < (slot_first + my_len)[None, :])
    live_slot = jnp.any(inside, axis=1)
    shard_ids = jnp.arange(shard_count, dtype=jnp.int32)
    source = lax.optimization_barrier(jnp.sum(jnp.where(inside, shard_ids[None, :], 0), axis=1)).astype(jnp.int32)
    token_index = (slot_ids - lax.optimization_barrier(jnp.sum(jnp.where(inside, slot_first[None, :], 0), axis=1))).astype(jnp.int32)
    shard_row = (lax.optimization_barrier(jnp.sum(jnp.where(inside, my_off[None, :], 0), axis=1)) + token_index).astype(jnp.int32)
    return (live_slot, source, token_index, shard_row)

def reference(lm_grad, image_tokens, image_offset, image_owner, mlp_input, layer_output, pre_gain, pre_bias, fc1_weight, fc1_bias, fc2_weight, post_gain, post_bias, merge_gain):

    def chip_step(running, chip_flat):
        replica = (chip_flat // SHARDS).astype(jnp.int32)
        chip_index = (chip_flat % SHARDS).astype(jnp.int32)
        lengths = lax.dynamic_index_in_dim(image_tokens, replica, 0, keepdims=False)
        offsets = lax.dynamic_index_in_dim(image_offset, replica, 0, keepdims=False)
        owners = lax.dynamic_index_in_dim(image_owner, replica, 0, keepdims=False)
        live_slot, source, token_index, shard_row = slot_source(lengths, offsets, owners, chip_index)
        global_row = jnp.clip(source * ROWS_DEV + shard_row, 0, SHARDS * ROWS_DEV - 1).astype(jnp.int32)
        replica_grad = lax.dynamic_index_in_dim(lm_grad, replica, 0, keepdims=False)
        picked = jnp.take(replica_grad, global_row, axis=1)
        incoming = jnp.where(live_slot[None, :, None], picked, jnp.zeros_like(picked))
        slot_start = (chip_index * CAP_TOK).astype(jnp.int32)
        layer_rows = lax.dynamic_slice_in_dim(lax.dynamic_index_in_dim(layer_output, replica, 0, keepdims=False), slot_start, CAP_TOK, 1)
        input_rows = lax.dynamic_slice_in_dim(lax.dynamic_index_in_dim(mlp_input, replica, 0, keepdims=False), slot_start, CAP_TOK, 1)
        res_grad, merge_grad, post_grad, shift_grad = head_back(incoming, layer_rows, merge_gain, post_gain, post_bias)
        res_wire = res_grad.astype(jnp.bfloat16)
        normed = (layer_norm(input_rows.astype(jnp.float32)) * pre_gain + pre_bias).astype(jnp.bfloat16)
        pre_act = jnp.dot(normed.reshape(-1, D), fc1_weight, preferred_element_type=jnp.float32) + fc1_bias
        hidden_grad = jnp.dot(res_wire.reshape(-1, D), fc2_weight.T, preferred_element_type=jnp.float32) * gelu_slope(pre_act)
        fc1_part = lax.optimization_barrier(jnp.sum(hidden_grad, axis=0))
        upstream = jnp.dot(hidden_grad.astype(jnp.bfloat16), fc1_weight.T, preferred_element_type=jnp.float32).reshape(PATCH_GROUP, CAP_TOK, D)
        input_grad, pre_scale_grad, pre_shift_grad = pre_back(input_rows, pre_gain, pre_bias, upstream)
        act_rows = (res_grad + input_grad).astype(jnp.bfloat16)
        fc2_part = lax.optimization_barrier(jnp.sum(res_grad, axis=(0, 1)))
        norm_part = jnp.stack([merge_grad, post_grad, shift_grad, fc2_part, pre_scale_grad, pre_shift_grad])
        return ((running[0] + norm_part, running[1] + fc1_part), act_rows)
    start_sums = (jnp.zeros((6, D), jnp.float32), jnp.zeros((FF,), jnp.float32))
    (norm_sum, fc1_sum), act_rows = lax.scan(chip_step, start_sums, jnp.arange(REPLICAS * SHARDS, dtype=jnp.int32))
    act_grad = act_rows.reshape(REPLICAS, SHARDS, PATCH_GROUP, CAP_TOK, D).transpose(0, 2, 1, 3, 4).reshape(REPLICAS, PATCH_GROUP, SHARDS * CAP_TOK, D)
    grad_scale = 1.0 / math.sqrt(PATCHES)
    return (act_grad, norm_sum * grad_scale, fc1_sum * grad_scale)
```

```python
import math

import jax
import jax.numpy as jnp
from jax import lax
from jax.experimental import pallas as pl
from jax.experimental.pallas import tpu as pltpu
from jax.sharding import PartitionSpec as P

WINDOW = 16
SUB = 8
LANES = 128
CHUNK = 512
PIECES = 3
EPSILON = 1e-06
SLOPE_K = math.sqrt(2.0 / math.pi)
CUBIC = 0.044715
F32 = jnp.float32
BF16 = jnp.bfloat16
MESH_ID = pl.DeviceIdType.MESH
NT = (((1,), (1,)), ((), ()))


def gelu_slope(pre_act):
    square = pre_act * pre_act
    tangent = jnp.tanh(pre_act * (SLOPE_K + (SLOPE_K * CUBIC) * square))
    half = 0.5 + 0.5 * tangent
    return half + half * (1.0 - tangent) * pre_act * (SLOPE_K + (3.0 * SLOPE_K * CUBIC) * square)


def row_mean(values):
    return jnp.mean(values, axis=-1, keepdims=True)


def norm_parts(values):
    centred = values - row_mean(values)
    scale = lax.rsqrt(row_mean(centred * centred) + EPSILON)
    return centred * scale, scale


def norm_pull(normal, scale, cotangent):
    return scale * (cotangent - row_mean(cotangent) - normal * row_mean(cotangent * normal))


def others(axis, count):
    me = lax.axis_index(axis)
    return [{axis: lax.rem(me + step, count)} for step in range(1, count)]


def remote(src, dst, send_sem, recv_sem, peer):
    copy = pltpu.make_async_remote_copy(
        src_ref=src,
        dst_ref=dst,
        send_sem=send_sem,
        recv_sem=recv_sem,
        device_id=peer,
        device_id_type=MESH_ID,
    )
    copy.start()
    return copy


def spans_of(total, step):
    return [(at, min(step, total - at)) for at in range(0, total, step)]


def col_sum(values):
    return jnp.sum(values, axis=0, keepdims=True)


def main_kernel(
    shards,
    replicas,
    grad_scale,
    tokens_hbm,
    offsets_hbm,
    owners_hbm,
    grad_hbm,
    layer_hbm,
    input_hbm,
    pre_gain_hbm,
    pre_bias_hbm,
    up_hbm,
    unit_bias_hbm,
    down_hbm,
    post_gain_hbm,
    post_bias_hbm,
    merge_hbm,
    act_ref,
    norm_ref,
    unit_ref,
    tokens_ref,
    offsets_ref,
    owners_ref,
    grad_ref,
    layer_ref,
    input_ref,
    pre_gain_ref,
    pre_bias_ref,
    up_ref,
    unit_bias_ref,
    down_ref,
    post_gain_ref,
    post_bias_ref,
    merge_ref,
    send_buf,
    recv_buf,
    normed,
    normals,
    scales,
    head_normal,
    head_unit,
    head_scale,
    head_rms,
    slopes,
    res_keep,
    res_out,
    res_in,
    hidden,
    part_keep,
    part_out,
    part_in,
    head_seq,
    head_dp,
    head_last,
    unit_seq,
    unit_dp,
    unit_last,
    late_seq,
    late_dp,
    late_last,
    load_sem,
    seq_send,
    seq_recv,
    enc_send,
    enc_recv,
    sum_send,
    sum_recv,
):
    me = lax.axis_index("seq")
    replica = lax.axis_index("dp")
    core = lax.axis_index("enc")
    other = 1 - core
    partner = {"enc": other}
    seq_peers = others("seq", shards)
    dp_peers = others("dp", replicas)
    peers = [partner] + seq_peers + dp_peers
    barrier = pltpu.get_barrier_semaphore()
    for peer in peers:
        pl.semaphore_signal(barrier, inc=1, device_id=peer, device_id_type=MESH_ID)

    blocks, tiles, own, width = layer_hbm.shape
    rows = blocks * SUB
    slots = blocks * tiles
    wide = res_out.shape[0]
    units = up_hbm.shape[0]
    unit_pad = up_ref.shape[0]
    rows_dev = grad_hbm.shape[0] // own
    images = tokens_hbm.shape[1]
    window = own * WINDOW
    places = shards * window
    chunks = spans_of(units, CHUNK)

    started = []

    def load(src, dst):
        copy = pltpu.make_async_copy(src, dst, load_sem.at[len(started)])
        copy.start()
        started.append(copy)
        return copy

    table_loads = [
        load(tokens_hbm, tokens_ref),
        load(offsets_hbm, offsets_ref),
        load(owners_hbm, owners_ref),
    ]
    grad_load = load(grad_hbm, grad_ref)
    input_loads = [
        [
            load(
                input_hbm.at[:, tile, pl.ds(half * own, own), :],
                input_ref.at[half, :, pl.ds(tile * own, own), :],
            )
            for tile in range(tiles)
        ]
        for half in range(2)
    ]
    pre_loads = [load(pre_gain_hbm, pre_gain_ref), load(pre_bias_hbm, pre_bias_ref)]
    bias_load = load(unit_bias_hbm, unit_bias_ref)
    up_loads = [load(up_hbm.at[pl.ds(at, size)], up_ref.at[pl.ds(at, size)]) for at, size in chunks]
    layer_loads = [
        load(layer_hbm.at[:, tile], layer_ref.at[:, pl.ds(tile * own, own), :]) for tile in range(tiles)
    ]
    post_loads = [
        load(post_gain_hbm, post_gain_ref),
        load(post_bias_hbm, post_bias_ref),
        load(merge_hbm, merge_ref),
    ]
    down_loads = [
        load(down_hbm.at[pl.ds(at, size)], down_ref.at[pl.ds(at, size)]) for at, size in chunks
    ]

    if unit_pad > units:
        up_ref[units:unit_pad, :] = jnp.zeros((unit_pad - units, width), BF16)
        hidden[:, :, units:unit_pad] = jnp.zeros((2, wide, unit_pad - units), BF16)
    if wide > rows:
        normed[:, rows:wide, :] = jnp.zeros((2, wide - rows, width), BF16)
        res_out[rows:wide, :] = jnp.zeros((wide - rows, width), BF16)

    for copy in table_loads:
        copy.wait()
    place = lax.broadcasted_iota(jnp.int32, (places, own * rows_dev), 0)
    chip, step = place // window, place % WINDOW
    patch = (place // WINDOW) % own
    source = jnp.full((places, own * rows_dev), -own * rows_dev, jnp.int32)
    for image in range(images):
        taken = (chip == owners_ref[me, image]) & (step < tokens_ref[me, image])
        source = jnp.where(taken, offsets_ref[me, image] + step, source)
    column = lax.broadcasted_iota(jnp.int32, (places, own * rows_dev), 1)
    pack = jnp.where(column == source + patch * rows_dev, 1.0, 0.0).astype(BF16)
    grad_load.wait()
    packed = jnp.dot(pack, grad_ref[...], preferred_element_type=F32)
    send_buf[...] = packed.astype(BF16).reshape(shards, window, width)
    pl.semaphore_wait(barrier, len(peers))
    token_copies = [
        remote(
            send_buf.at[peer["seq"]], recv_buf.at[me], seq_send.at[index], seq_recv.at[index], peer
        )
        for index, peer in enumerate(seq_peers)
    ]
    recv_buf[me] = send_buf[me]

    for copy in pre_loads:
        copy.wait()
    pre_gain = pre_gain_ref[...].reshape(1, -1)
    pre_bias = pre_bias_ref[...].reshape(1, -1)
    for half in range(2):
        for copy in input_loads[half]:
            copy.wait()
        for block in range(blocks):
            normal, scale = norm_parts(input_ref[half, block].astype(F32))
            normals[half, block] = normal
            scales[half, block] = jnp.broadcast_to(scale, (SUB, LANES))
            normed[half, block * SUB : (block + 1) * SUB, :] = (normal * pre_gain + pre_bias).astype(BF16)

    for copy in layer_loads + post_loads:
        copy.wait()
    post_gain = post_gain_ref[...].reshape(1, -1)
    post_bias = post_bias_ref[...].reshape(1, -1)
    merge_gain = merge_ref[...].reshape(1, -1)
    for block in range(blocks):
        normal, scale = norm_parts(layer_ref[block].astype(F32))
        affine = normal * post_gain + post_bias
        rms = lax.rsqrt(row_mean(affine * affine) + EPSILON)
        head_normal[block] = normal
        head_unit[block] = affine * rms
        head_scale[block] = jnp.broadcast_to(scale, (SUB, LANES))
        head_rms[block] = jnp.broadcast_to(rms, (SUB, LANES))

    place = lax.broadcasted_iota(jnp.int32, (rows, places), 1)
    chip, step = place // window, place % WINDOW
    patch = (place // WINDOW) % own
    target = jnp.full((rows, places), -1, jnp.int32)
    first = jnp.int32(0)
    for shard in range(shards):
        count = jnp.int32(0)
        for image in range(images):
            count += jnp.where(owners_ref[shard, image] == me, tokens_ref[shard, image], 0)
        target = jnp.where((chip == shard) & (step < count), (first + step) * own + patch, target)
        first += count
    row = lax.broadcasted_iota(jnp.int32, (rows, places), 0)
    unpack = jnp.where(row == target, 1.0, 0.0).astype(BF16)

    bias_load.wait()
    unit_bias = unit_bias_ref[...].reshape(1, -1)
    for (at, size), copy in zip(chunks, up_loads):
        copy.wait()
        for half in range(2):
            pre_act = lax.dot_general(
                normed[half], up_ref[at : at + size, :], NT, preferred_element_type=F32
            )
            slopes[half, :, at : at + size] = gelu_slope(pre_act + unit_bias[:, at : at + size])

    for copy in token_copies:
        copy.wait()
    landed = recv_buf[...].reshape(places, width)
    incoming_all = jnp.dot(unpack, landed, preferred_element_type=F32)
    totals = None
    for block in range(blocks):
        incoming = incoming_all[block * SUB : (block + 1) * SUB, :]
        normal = head_normal[block]
        unit = head_unit[block]
        scale = head_scale[block][:, 0:1]
        rms = head_rms[block][:, 0:1]
        unit_grad = incoming * merge_gain
        affine_grad = rms * (unit_grad - unit * row_mean(unit_grad * unit))
        res = norm_pull(normal, scale, affine_grad * post_gain)
        res_keep[block] = res
        res_out[block * SUB : (block + 1) * SUB, :] = res.astype(BF16)
        parts = [incoming * unit, affine_grad * normal, affine_grad, res]
        totals = parts if totals is None else [a + b for a, b in zip(totals, parts)]
    res_copy = remote(res_out, res_in, enc_send.at[0], enc_recv.at[0], partner)
    for index, total in enumerate(totals):
        head_seq[me, index : index + 1, :] = col_sum(total)

    sums = []

    def gather(buffer, place, axis_peers):
        copies = [
            remote(
                buffer.at[place],
                buffer.at[place],
                sum_send.at[len(sums) + index],
                sum_recv.at[len(sums) + index],
                peer,
            )
            for index, peer in enumerate(axis_peers)
        ]
        sums.extend(copies)
        return copies

    def settle(copies, buffer, count):
        for copy in copies:
            copy.wait()
        total = buffer[0]
        for index in range(1, count):
            total = total + buffer[index]
        return total

    head_copies = gather(head_seq, me, seq_peers)

    unit_rows = spans_of(units, width)
    unit_sums = []

    def down_half(half, res):
        for index, (at, size) in enumerate(chunks):
            if len(unit_sums) < len(chunks):
                down_loads[index].wait()
            back = lax.dot_general(res, down_ref[at : at + size, :], NT, preferred_element_type=F32)
            grads = back * slopes[half, :, at : at + size]
            hidden[half, :, at : at + size] = grads.astype(BF16)
            partial = col_sum(grads)
            if len(unit_sums) < len(chunks):
                unit_sums.append(partial)
            else:
                unit_sums[index] = unit_sums[index] + partial

    down_half(core, res_out[...])
    res_copy.wait()
    down_half(other, res_in[...])
    unit_seq[me] = jnp.zeros(unit_seq.shape[1:], F32)
    unit_total = jnp.concatenate(unit_sums, axis=1)
    for index, (at, size) in enumerate(unit_rows):
        unit_seq[me, index : index + 1, 0:size] = unit_total[:, at : at + size]
    unit_copies = gather(unit_seq, me, seq_peers)

    pieces = spans_of(width, width // PIECES)
    part_copies = []
    hidden_other = hidden[other]
    for index, (at, size) in enumerate(pieces):
        part = jnp.dot(hidden_other, up_ref[:, at : at + size], preferred_element_type=F32)
        part_keep[0, :, at : at + size] = part
        part_out[index] = part.astype(BF16)
        part_copies.append(
            remote(
                part_out.at[index],
                part_in.at[index],
                enc_send.at[1 + index],
                enc_recv.at[1 + index],
                partner,
            )
        )
    head_dp[replica] = settle(head_copies, head_seq, shards)
    head_copies = gather(head_dp, replica, dp_peers)
    hidden_own = hidden[core]
    for at, size in pieces:
        part_keep[1, :, at : at + size] = jnp.dot(
            hidden_own, up_ref[:, at : at + size], preferred_element_type=F32
        )
    totals = None
    for index, half in enumerate((other, core)):
        for block in range(blocks):
            part = part_keep[index, block * SUB : (block + 1) * SUB, :]
            parts = [part * normals[half, block], part]
            totals = parts if totals is None else [a + b for a, b in zip(totals, parts)]
    for index, total in enumerate(totals):
        late_seq[me, index : index + 1, :] = col_sum(total)
    late_copies = gather(late_seq, me, seq_peers)
    unit_dp[replica] = settle(unit_copies, unit_seq, shards)
    unit_copies = gather(unit_dp, replica, dp_peers)

    for copy in part_copies:
        copy.wait()
    for block in range(blocks):
        span = slice(block * SUB, (block + 1) * SUB)
        theirs = jnp.concatenate([part_in[index, span, :] for index in range(len(pieces))], axis=1)
        upstream = part_keep[1, span, :] + theirs.astype(F32)
        act = res_keep[block] + norm_pull(
            normals[core, block], scales[core, block][:, 0:1], upstream * pre_gain
        )
        act_ref[block] = act.astype(BF16)

    late_dp[replica] = settle(late_copies, late_seq, shards)
    late_copies = gather(late_dp, replica, dp_peers)
    head_last[core] = settle(head_copies, head_dp, replicas)
    unit_last[core] = settle(unit_copies, unit_dp, replicas) * grad_scale
    head_copies = gather(head_last, core, [partner])
    unit_copies = gather(unit_last, core, [partner])
    late_last[core] = settle(late_copies, late_dp, replicas)
    late_copies = gather(late_last, core, [partner])
    norm_ref[0:4, :] = settle(head_copies, head_last, 2) * grad_scale
    for copy in unit_copies:
        copy.wait()
    for half in range(2):
        for index, (at, size) in enumerate(unit_rows):
            unit_ref[half : half + 1, at : at + size] = unit_last[half, index : index + 1, 0:size]
    norm_ref[4:6, :] = settle(late_copies, late_last, 2) * grad_scale


def write_kernel(act_ref, norm_ref, unit_ref, act_hbm, norm_hbm, unit_hbm, flat, sems):
    tiles, own = act_hbm.shape[1:3]
    copies = [
        pltpu.make_async_copy(
            act_ref.at[:, pl.ds(tile * own, own), :], act_hbm.at[:, tile], sems.at[tile]
        )
        for tile in range(tiles)
    ]
    copies.append(pltpu.make_async_copy(norm_ref, norm_hbm, sems.at[tiles]))
    for copy in copies:
        copy.start()
    flat[...] = jnp.concatenate([unit_ref[0:1, :], unit_ref[1:2, :]], axis=1).reshape(-1)
    last = pltpu.make_async_copy(flat, unit_hbm, sems.at[tiles + 1])
    last.start()
    for copy in copies + [last]:
        copy.wait()


def round_up(value, step):
    return (value + step - 1) // step * step


def body(
    lm_grad,
    image_tokens,
    image_offset,
    image_owner,
    mlp_input,
    layer_output,
    pre_gain,
    pre_bias,
    fc1_weight,
    fc1_bias,
    fc2_weight,
    post_gain,
    post_bias,
    merge_gain,
):
    shards = lax.axis_size("seq")
    replicas = lax.axis_size("dp")
    cores = lax.axis_size("enc")
    own, rows_dev, width = lm_grad.shape[1:]
    group, slots = mlp_input.shape[1:3]
    images = image_tokens.shape[2]
    units = fc1_bias.shape[0]
    tiles = SUB // own
    blocks = slots // tiles
    rows = blocks * SUB
    wide = round_up(rows, 2 * SUB)
    unit_pad = round_up(units, LANES)
    unit_rows = round_up(units, width) // width
    chunk_count = len(spans_of(units, CHUNK))
    grad_scale = 1.0 / math.sqrt(group * rows_dev * shards * replicas)

    hbm = pl.BlockSpec(memory_space=pl.ANY)
    vmem = pl.BlockSpec(memory_space=pltpu.VMEM)
    dma = pltpu.SemaphoreType.DMA
    smem = pltpu.SMEM((shards, images), jnp.int32)
    piece = width // PIECES

    def main_call(*refs):
        main_kernel(shards, replicas, grad_scale, *refs)

    vector = pltpu.VMEM((width,), F32)
    sum_count = 3 * (shards - 1 + replicas - 1 + 1)
    act, norms, unit_sums = pl.pallas_call(
        main_call,
        out_shape=(
            jax.ShapeDtypeStruct((blocks, SUB, width), BF16),
            jax.ShapeDtypeStruct((6, width), F32),
            jax.ShapeDtypeStruct((cores, units), F32),
        ),
        in_specs=[hbm] * 14,
        out_specs=(vmem,) * 3,
        scratch_shapes=[
            smem,
            smem,
            smem,
            pltpu.VMEM((own * rows_dev, width), BF16),
            pltpu.VMEM((blocks, SUB, width), BF16),
            pltpu.VMEM((cores, blocks, SUB, width), BF16),
            vector,
            vector,
            pltpu.VMEM((unit_pad, width), BF16),
            pltpu.VMEM((units,), F32),
            pltpu.VMEM((unit_pad, width), BF16),
            vector,
            vector,
            vector,
            pltpu.VMEM((shards, own * WINDOW, width), BF16),
            pltpu.VMEM((shards, own * WINDOW, width), BF16),
            pltpu.VMEM((cores, wide, width), BF16),
            pltpu.VMEM((cores, blocks, SUB, width), F32),
            pltpu.VMEM((cores, blocks, SUB, LANES), F32),
            pltpu.VMEM((blocks, SUB, width), F32),
            pltpu.VMEM((blocks, SUB, width), F32),
            pltpu.VMEM((blocks, SUB, LANES), F32),
            pltpu.VMEM((blocks, SUB, LANES), F32),
            pltpu.VMEM((cores, wide, unit_pad), F32),
            pltpu.VMEM((blocks, SUB, width), F32),
            pltpu.VMEM((wide, width), BF16),
            pltpu.VMEM((wide, width), BF16),
            pltpu.VMEM((cores, wide, unit_pad), BF16),
            pltpu.VMEM((cores, wide, width), F32),
            pltpu.VMEM((PIECES, wide, piece), BF16),
            pltpu.VMEM((PIECES, wide, piece), BF16),
            pltpu.VMEM((shards, 4, width), F32),
            pltpu.VMEM((replicas, 4, width), F32),
            pltpu.VMEM((cores, 4, width), F32),
            pltpu.VMEM((shards, unit_rows, width), F32),
            pltpu.VMEM((replicas, unit_rows, width), F32),
            pltpu.VMEM((cores, unit_rows, width), F32),
            pltpu.VMEM((shards, 2, width), F32),
            pltpu.VMEM((replicas, 2, width), F32),
            pltpu.VMEM((cores, 2, width), F32),
            dma((10 + 3 * tiles + 2 * chunk_count,)),
            dma((shards - 1,)),
            dma((shards - 1,)),
            dma((1 + PIECES,)),
            dma((1 + PIECES,)),
            dma((sum_count,)),
            dma((sum_count,)),
        ],
        compiler_params=pltpu.CompilerParams(
            collective_id=0, has_side_effects=True, vmem_limit_bytes=48 * 1024 * 1024
        ),
        name="main",
    )(*[pltpu.with_memory_space_constraint(operand, pltpu.HBM) for operand in (
        image_tokens[0],
        image_offset[0],
        image_owner[0],
        lm_grad[0].reshape(own * rows_dev, width),
        layer_output[0].transpose(1, 0, 2).reshape(blocks, tiles, own, width),
        mlp_input[0].transpose(1, 0, 2).reshape(blocks, tiles, group, width),
        pre_gain,
        pre_bias,
        fc1_weight.T,
        fc1_bias,
        fc2_weight,
        post_gain,
        post_bias,
        merge_gain,
    )])

    act_grad, norm_grads, unit_grads = pl.pallas_call(
        write_kernel,
        out_shape=(
            jax.ShapeDtypeStruct((blocks, tiles, own, width), BF16),
            jax.ShapeDtypeStruct((6, width), F32),
            jax.ShapeDtypeStruct((cores * units,), F32),
        ),
        in_specs=[vmem] * 3,
        out_specs=(hbm,) * 3,
        scratch_shapes=[pltpu.VMEM((cores * units,), F32), dma((tiles + 2,))],
        compiler_params=pltpu.CompilerParams(vmem_limit_bytes=4 * 1024 * 1024),
        name="write",
    )(act, norms, unit_sums)
    act_grad = act_grad.reshape(slots, own, width).transpose(1, 0, 2)
    return (act_grad[None], norm_grads, unit_grads)


def solution(mesh):
    in_specs = (
        P("dp", "enc", "seq", None),
        P("dp", None, None),
        P("dp", None, None),
        P("dp", None, None),
        P("dp", None, "seq", None),
        P("dp", "enc", "seq", None),
        P(),
        P(),
        P(None, "enc"),
        P("enc"),
        P("enc", None),
        P(),
        P(),
        P(),
    )
    out_specs = (P("dp", "enc", "seq", None), P(), P())
    return jax.shard_map(body, mesh=mesh, in_specs=in_specs, out_specs=out_specs, check_vma=False)
```

```python
import math

import jax
import jax.numpy as jnp
from jax import lax
from jax.experimental import pallas as pl
from jax.experimental.pallas import tpu as pltpu
from jax.sharding import PartitionSpec as P

WINDOW = 16
SUB = 8
LANES = 128
CHUNK = 256
PIECE = 512
EPSILON = 1e-06
SLOPE_K = math.sqrt(2.0 / math.pi)
CUBIC = 0.044715
F32 = jnp.float32
BF16 = jnp.bfloat16
MESH_ID = pl.DeviceIdType.MESH
NT = (((1,), (1,)), ((), ()))


def gelu_slope(pre_act):
    inner = pre_act * (SLOPE_K + (SLOPE_K * CUBIC) * (pre_act * pre_act))
    half = 0.5 + 0.5 * jnp.tanh(inner)
    return half * (1.0 + (1.0 - half) * (6.0 * inner - (4.0 * SLOPE_K) * pre_act))


def row_mean(values):
    return jnp.mean(values, axis=-1, keepdims=True)


def norm_parts(values):
    centred = values - row_mean(values)
    scale = lax.rsqrt(row_mean(centred * centred) + EPSILON)
    return centred * scale, scale


def norm_pull(normal, scale, cotangent):
    return scale * (cotangent - row_mean(cotangent) - normal * row_mean(cotangent * normal))


def others(axis, count):
    me = lax.axis_index(axis)
    return [{axis: lax.rem(me + step, count)} for step in range(1, count)]


def remote(src, dst, send_sem, recv_sem, peer):
    copy = pltpu.make_async_remote_copy(
        src_ref=src,
        dst_ref=dst,
        send_sem=send_sem,
        recv_sem=recv_sem,
        device_id=peer,
        device_id_type=MESH_ID,
    )
    copy.start()
    return copy


def mesh_others(axis, count, cores):
    me = lax.axis_index(axis)
    core = lax.axis_index("enc")
    return [
        {axis: lax.rem(me + step, count), "enc": lax.rem(core + flip, cores)}
        for step in range(count)
        for flip in range(cores)
        if step + flip > 0
    ]


def spans_of(total, step):
    return [(at, min(step, total - at)) for at in range(0, total, step)]


def col_sum(values):
    return jnp.sum(values, axis=0, keepdims=True)


def main_kernel(
    shards,
    replicas,
    grad_scale,
    tokens_hbm,
    offsets_hbm,
    owners_hbm,
    grad_hbm,
    layer_hbm,
    input_hbm,
    pre_gain_hbm,
    pre_bias_hbm,
    up_hbm,
    unit_bias_hbm,
    down_hbm,
    post_gain_hbm,
    post_bias_hbm,
    merge_hbm,
    act_ref,
    norm_ref,
    unit_ref,
    tokens_ref,
    offsets_ref,
    owners_ref,
    grad_ref,
    layer_ref,
    input_ref,
    pre_gain_ref,
    pre_bias_ref,
    up_ref,
    unit_bias_ref,
    down_ref,
    post_gain_ref,
    post_bias_ref,
    merge_ref,
    send_buf,
    recv_buf,
    normed,
    normals,
    scales,
    head_normal,
    head_unit,
    head_scale,
    head_rms,
    slopes,
    res_keep,
    res_all,
    hidden,
    part_keep,
    part_out,
    part_in,
    head_seq,
    head_dp,
    head_last,
    unit_seq,
    unit_dp,
    unit_last,
    late_seq,
    late_total,
    late_dp,
    load_sem,
    seq_send,
    seq_recv,
    enc_send,
    enc_recv,
    sum_send,
    sum_recv,
    late_send,
    late_recv,
):
    me = lax.axis_index("seq")
    replica = lax.axis_index("dp")
    core = lax.axis_index("enc")
    other = 1 - core
    partner = {"enc": other}
    seq_peers = others("seq", shards)
    dp_peers = others("dp", replicas)
    seq_all = mesh_others("seq", shards, 2)
    dp_all = mesh_others("dp", replicas, 2)
    greeted = seq_all + [peer for index, peer in enumerate(dp_all) if index > 0]
    barrier = pltpu.get_barrier_semaphore()
    for peer in greeted:
        pl.semaphore_signal(barrier, inc=1, device_id=peer, device_id_type=MESH_ID)

    blocks, tiles, own, width = layer_hbm.shape
    rows = blocks * SUB
    slots = blocks * tiles
    wide = res_all.shape[1]
    units = up_hbm.shape[0]
    unit_pad = up_ref.shape[0]
    rows_dev = grad_hbm.shape[0] // own
    images = tokens_hbm.shape[1]
    window = own * WINDOW
    places = shards * window
    chunks = spans_of(units, CHUNK)

    started = []

    def load(src, dst):
        copy = pltpu.make_async_copy(src, dst, load_sem.at[len(started)])
        copy.start()
        started.append(copy)
        return copy

    table_loads = [
        load(tokens_hbm, tokens_ref),
        load(offsets_hbm, offsets_ref),
        load(owners_hbm, owners_ref),
    ]
    grad_load = load(grad_hbm, grad_ref)
    input_loads = [
        [
            load(
                input_hbm.at[:, tile, pl.ds(half * own, own), :],
                input_ref.at[half, :, pl.ds(tile * own, own), :],
            )
            for tile in range(tiles)
        ]
        for half in range(2)
    ]
    pre_loads = [load(pre_gain_hbm, pre_gain_ref), load(pre_bias_hbm, pre_bias_ref)]
    bias_load = load(unit_bias_hbm, unit_bias_ref)
    up_loads = [load(up_hbm.at[pl.ds(at, size)], up_ref.at[pl.ds(at, size)]) for at, size in chunks]
    layer_loads = [
        load(layer_hbm.at[:, tile], layer_ref.at[:, pl.ds(tile * own, own), :]) for tile in range(tiles)
    ]
    post_loads = [
        load(post_gain_hbm, post_gain_ref),
        load(post_bias_hbm, post_bias_ref),
        load(merge_hbm, merge_ref),
    ]
    down_loads = [
        load(down_hbm.at[pl.ds(at, size)], down_ref.at[pl.ds(at, size)]) for at, size in chunks
    ]

    if unit_pad > units:
        up_ref[units:unit_pad, :] = jnp.zeros((unit_pad - units, width), BF16)
        hidden[:, units:unit_pad] = jnp.zeros((2 * wide, unit_pad - units), BF16)
    if wide > rows:
        normed[:, rows:wide, :] = jnp.zeros((2, wide - rows, width), BF16)
        res_all[core, rows:wide, :] = jnp.zeros((wide - rows, width), BF16)

    for copy in table_loads:
        copy.wait()
    place = lax.broadcasted_iota(jnp.int32, (places, own * rows_dev), 0)
    chip, step = place // window, place % WINDOW
    patch = (place // WINDOW) % own
    source = jnp.full((places, own * rows_dev), -own * rows_dev, jnp.int32)
    for image in range(images):
        taken = (chip == owners_ref[me, image]) & (step < tokens_ref[me, image])
        source = jnp.where(taken, offsets_ref[me, image] + step, source)
    column = lax.broadcasted_iota(jnp.int32, (places, own * rows_dev), 1)
    pack = jnp.where(column == source + patch * rows_dev, 1.0, 0.0).astype(BF16)
    grad_load.wait()
    packed = jnp.dot(pack, grad_ref[...], preferred_element_type=F32)
    send_buf[...] = packed.astype(BF16).reshape(shards, window, width)
    pl.semaphore_wait(barrier, len(greeted))
    token_copies = [
        remote(
            send_buf.at[peer["seq"]], recv_buf.at[me], seq_send.at[index], seq_recv.at[index], peer
        )
        for index, peer in enumerate(seq_peers)
    ]
    recv_buf[me] = send_buf[me]

    for copy in pre_loads:
        copy.wait()
    pre_gain = pre_gain_ref[...].reshape(1, -1)
    pre_bias = pre_bias_ref[...].reshape(1, -1)
    for half in range(2):
        for copy in input_loads[half]:
            copy.wait()
        for block in range(blocks):
            normal, scale = norm_parts(input_ref[half, block].astype(F32))
            normals[half, block] = normal
            scales[half, block] = jnp.broadcast_to(scale, (SUB, LANES))
            normed[half, block * SUB : (block + 1) * SUB, :] = (normal * pre_gain + pre_bias).astype(BF16)

    for copy in layer_loads + post_loads:
        copy.wait()
    post_gain = post_gain_ref[...].reshape(1, -1)
    post_bias = post_bias_ref[...].reshape(1, -1)
    merge_gain = merge_ref[...].reshape(1, -1)
    for block in range(blocks):
        normal, scale = norm_parts(layer_ref[block].astype(F32))
        affine = normal * post_gain + post_bias
        rms = lax.rsqrt(row_mean(affine * affine) + EPSILON)
        head_normal[block] = normal
        head_unit[block] = affine * rms
        head_scale[block] = jnp.broadcast_to(scale, (SUB, LANES))
        head_rms[block] = jnp.broadcast_to(rms, (SUB, LANES))

    place = lax.broadcasted_iota(jnp.int32, (rows, places), 1)
    chip, step = place // window, place % WINDOW
    patch = (place // WINDOW) % own
    target = jnp.full((rows, places), -1, jnp.int32)
    first = jnp.int32(0)
    for shard in range(shards):
        count = jnp.int32(0)
        for image in range(images):
            count += jnp.where(owners_ref[shard, image] == me, tokens_ref[shard, image], 0)
        target = jnp.where((chip == shard) & (step < count), (first + step) * own + patch, target)
        first += count
    row = lax.broadcasted_iota(jnp.int32, (rows, places), 0)
    unpack = jnp.where(row == target, 1.0, 0.0).astype(BF16)

    bias_load.wait()
    unit_bias = unit_bias_ref[...].reshape(1, -1)
    for copy in up_loads:
        copy.wait()
    normed_all = normed[...].reshape(2 * wide, width)
    for at, size in chunks:
        pre_act = lax.dot_general(
            normed_all, up_ref[at : at + size, :], NT, preferred_element_type=F32
        )
        slopes[:, at : at + size] = gelu_slope(pre_act + unit_bias[:, at : at + size])

    for copy in token_copies:
        copy.wait()
    landed = recv_buf[...].reshape(places, width)
    incoming_all = jnp.dot(unpack, landed, preferred_element_type=F32)
    totals = None
    for block in range(blocks):
        incoming = incoming_all[block * SUB : (block + 1) * SUB, :]
        normal = head_normal[block]
        unit = head_unit[block]
        scale = head_scale[block][:, 0:1]
        rms = head_rms[block][:, 0:1]
        unit_grad = incoming * merge_gain
        affine_grad = rms * (unit_grad - unit * row_mean(unit_grad * unit))
        res = norm_pull(normal, scale, affine_grad * post_gain)
        res_keep[block] = res
        res_all[core, block * SUB : (block + 1) * SUB, :] = res.astype(BF16)
        parts = [incoming * unit, affine_grad * normal, affine_grad, res]
        totals = parts if totals is None else [a + b for a, b in zip(totals, parts)]
    res_copy = remote(res_all.at[core], res_all.at[core], enc_send.at[0], enc_recv.at[0], partner)
    for index, total in enumerate(totals):
        head_seq[me, index : index + 1, :] = col_sum(total)

    sums = []

    def gather(buffer, place, axis_peers):
        copies = [
            remote(
                buffer.at[place],
                buffer.at[place],
                sum_send.at[len(sums) + index],
                sum_recv.at[len(sums) + index],
                peer,
            )
            for index, peer in enumerate(axis_peers)
        ]
        sums.extend(copies)
        return copies

    def settle(copies, buffer, count):
        for copy in copies:
            copy.wait()
        total = buffer[0]
        for index in range(1, count):
            total = total + buffer[index]
        return total

    head_copies = gather(head_seq, me, seq_peers)

    unit_rows = spans_of(units, width)
    unit_sums = []
    for copy in down_loads:
        copy.wait()
    res_copy.wait()
    res_rows = res_all[...].reshape(2 * wide, width)
    for at, size in chunks:
        back = lax.dot_general(
            res_rows, down_ref[at : at + size, :], NT, preferred_element_type=F32
        )
        grads = back * slopes[:, at : at + size]
        hidden[:, at : at + size] = grads.astype(BF16)
        unit_sums.append(col_sum(grads))
    unit_seq[me] = jnp.zeros(unit_seq.shape[1:], F32)
    unit_total = jnp.concatenate(unit_sums, axis=1)
    for index, (at, size) in enumerate(unit_rows):
        unit_seq[me, index : index + 1, 0:size] = unit_total[:, at : at + size]
    unit_copies = gather(unit_seq, me, seq_peers)

    pieces = spans_of(width, PIECE)
    part_copies = []
    hidden_all = hidden[...]
    for index, (at, size) in enumerate(pieces):
        span = slice(at, at + size)
        part = jnp.dot(hidden_all, up_ref[:, span], preferred_element_type=F32)
        part_keep[:, :, span] = part.reshape(2, wide, size)
        part_out[:, span] = part_keep[other, :, span].astype(BF16)
        part_copies.append(
            remote(
                part_out.at[:, pl.ds(at, size)],
                part_in.at[:, pl.ds(at, size)],
                enc_send.at[1 + index],
                enc_recv.at[1 + index],
                partner,
            )
        )
        gain_sum = None
        for half in range(2):
            for block in range(blocks):
                at_row = half * wide + block * SUB
                block_part = part[at_row : at_row + SUB, :]
                term = block_part * normals[half, block, :, span]
                gain_sum = term if gain_sum is None else gain_sum + term
                bias_sum = block_part if half + block == 0 else bias_sum + block_part
        late_seq[me, core, 0:1, span] = col_sum(gain_sum)
        late_seq[me, core, 1:2, span] = col_sum(bias_sum)
    late_copies = [
        remote(
            late_seq.at[me, core], late_seq.at[me, core], late_send.at[index], late_recv.at[index], peer
        )
        for index, peer in enumerate(seq_all)
    ]
    head_dp[replica] = settle(head_copies, head_seq, shards)
    head_copies = gather(head_dp, replica, dp_peers)
    unit_dp[replica] = settle(unit_copies, unit_seq, shards)
    unit_copies = gather(unit_dp, replica, dp_peers)

    for copy in part_copies:
        copy.wait()
    for block in range(blocks):
        span = slice(block * SUB, (block + 1) * SUB)
        upstream = part_keep[core, span, :] + part_in[span, :].astype(F32)
        act = res_keep[block] + norm_pull(
            normals[core, block], scales[core, block][:, 0:1], upstream * pre_gain
        )
        act_ref[block] = act.astype(BF16)

    for copy in late_copies:
        copy.wait()
    total = None
    for shard in range(shards):
        for half in range(2):
            term = late_seq[shard, half]
            total = term if total is None else total + term
    total = total * grad_scale
    late_total[0] = total[0:1, :]
    late_total[1] = total[1:2, :]
    late_dp[replica, core] = late_total[core]
    base = len(seq_all)
    late_copies = [
        remote(
            late_total.at[core],
            late_dp.at[replica, core],
            late_send.at[base + index],
            late_recv.at[base + index],
            peer,
        )
        for index, peer in enumerate(dp_all)
    ]
    head_last[core] = settle(head_copies, head_dp, replicas)
    unit_last[core] = settle(unit_copies, unit_dp, replicas) * grad_scale
    head_copies = gather(head_last, core, [partner])
    unit_copies = gather(unit_last, core, [partner])
    norm_ref[0:4, :] = settle(head_copies, head_last, 2) * grad_scale
    for copy in unit_copies:
        copy.wait()
    for half in range(2):
        for index, (at, size) in enumerate(unit_rows):
            unit_ref[half : half + 1, at : at + size] = unit_last[half, index : index + 1, 0:size]
    for copy in late_copies:
        copy.wait()
    for half in range(2):
        total = late_dp[0, half]
        for index in range(1, replicas):
            total = total + late_dp[index, half]
        norm_ref[4 + half : 5 + half, :] = total


def write_kernel(act_ref, norm_ref, unit_ref, act_hbm, norm_hbm, unit_hbm, flat, sems):
    tiles, own = act_hbm.shape[1:3]
    copies = [
        pltpu.make_async_copy(
            act_ref.at[:, pl.ds(tile * own, own), :], act_hbm.at[:, tile], sems.at[tile]
        )
        for tile in range(tiles)
    ]
    copies.append(pltpu.make_async_copy(norm_ref, norm_hbm, sems.at[tiles]))
    for copy in copies:
        copy.start()
    flat[...] = jnp.concatenate([unit_ref[0:1, :], unit_ref[1:2, :]], axis=1).reshape(-1)
    last = pltpu.make_async_copy(flat, unit_hbm, sems.at[tiles + 1])
    last.start()
    for copy in copies + [last]:
        copy.wait()


def round_up(value, step):
    return (value + step - 1) // step * step


def body(
    lm_grad,
    image_tokens,
    image_offset,
    image_owner,
    mlp_input,
    layer_output,
    pre_gain,
    pre_bias,
    fc1_weight,
    fc1_bias,
    fc2_weight,
    post_gain,
    post_bias,
    merge_gain,
):
    shards = lax.axis_size("seq")
    replicas = lax.axis_size("dp")
    cores = lax.axis_size("enc")
    own, rows_dev, width = lm_grad.shape[1:]
    group, slots = mlp_input.shape[1:3]
    images = image_tokens.shape[2]
    units = fc1_bias.shape[0]
    tiles = SUB // own
    blocks = slots // tiles
    rows = blocks * SUB
    wide = round_up(rows, 2 * SUB)
    unit_pad = round_up(units, LANES)
    unit_rows = round_up(units, width) // width
    chunk_count = len(spans_of(units, CHUNK))
    grad_scale = 1.0 / math.sqrt(group * rows_dev * shards * replicas)

    hbm = pl.BlockSpec(memory_space=pl.ANY)
    vmem = pl.BlockSpec(memory_space=pltpu.VMEM)
    dma = pltpu.SemaphoreType.DMA
    smem = pltpu.SMEM((shards, images), jnp.int32)
    piece_count = len(spans_of(width, PIECE))

    def main_call(*refs):
        main_kernel(shards, replicas, grad_scale, *refs)

    vector = pltpu.VMEM((width,), F32)
    sum_count = 2 * (shards - 1 + replicas - 1 + 1)
    late_count = cores * (shards + replicas) - 2
    act, norms, unit_sums = pl.pallas_call(
        main_call,
        out_shape=(
            jax.ShapeDtypeStruct((blocks, SUB, width), BF16),
            jax.ShapeDtypeStruct((6, width), F32),
            jax.ShapeDtypeStruct((cores, units), F32),
        ),
        in_specs=[hbm] * 14,
        out_specs=(vmem,) * 3,
        scratch_shapes=[
            smem,
            smem,
            smem,
            pltpu.VMEM((own * rows_dev, width), BF16),
            pltpu.VMEM((blocks, SUB, width), BF16),
            pltpu.VMEM((cores, blocks, SUB, width), BF16),
            vector,
            vector,
            pltpu.VMEM((unit_pad, width), BF16),
            pltpu.VMEM((units,), F32),
            pltpu.VMEM((unit_pad, width), BF16),
            vector,
            vector,
            vector,
            pltpu.VMEM((shards, own * WINDOW, width), BF16),
            pltpu.VMEM((shards, own * WINDOW, width), BF16),
            pltpu.VMEM((cores, wide, width), BF16),
            pltpu.VMEM((cores, blocks, SUB, width), F32),
            pltpu.VMEM((cores, blocks, SUB, LANES), F32),
            pltpu.VMEM((blocks, SUB, width), F32),
            pltpu.VMEM((blocks, SUB, width), F32),
            pltpu.VMEM((blocks, SUB, LANES), F32),
            pltpu.VMEM((blocks, SUB, LANES), F32),
            pltpu.VMEM((cores * wide, unit_pad), F32),
            pltpu.VMEM((blocks, SUB, width), F32),
            pltpu.VMEM((cores, wide, width), BF16),
            pltpu.VMEM((cores * wide, unit_pad), BF16),
            pltpu.VMEM((cores, wide, width), F32),
            pltpu.VMEM((wide, width), BF16),
            pltpu.VMEM((wide, width), BF16),
            pltpu.VMEM((shards, 4, width), F32),
            pltpu.VMEM((replicas, 4, width), F32),
            pltpu.VMEM((cores, 4, width), F32),
            pltpu.VMEM((shards, unit_rows, width), F32),
            pltpu.VMEM((replicas, unit_rows, width), F32),
            pltpu.VMEM((cores, unit_rows, width), F32),
            pltpu.VMEM((shards, cores, 2, width), F32),
            pltpu.VMEM((cores, 1, width), F32),
            pltpu.VMEM((replicas, cores, 1, width), F32),
            dma((10 + 3 * tiles + 2 * chunk_count,)),
            dma((shards - 1,)),
            dma((shards - 1,)),
            dma((1 + piece_count,)),
            dma((1 + piece_count,)),
            dma((sum_count,)),
            dma((sum_count,)),
            dma((late_count,)),
            dma((late_count,)),
        ],
        compiler_params=pltpu.CompilerParams(
            collective_id=0, has_side_effects=True, vmem_limit_bytes=48 * 1024 * 1024
        ),
        name="main",
    )(*[pltpu.with_memory_space_constraint(operand, pltpu.HBM) for operand in (
        image_tokens[0],
        image_offset[0],
        image_owner[0],
        lm_grad[0].reshape(own * rows_dev, width),
        layer_output[0].transpose(1, 0, 2).reshape(blocks, tiles, own, width),
        mlp_input[0].transpose(1, 0, 2).reshape(blocks, tiles, group, width),
        pre_gain,
        pre_bias,
        fc1_weight.T,
        fc1_bias,
        fc2_weight,
        post_gain,
        post_bias,
        merge_gain,
    )])

    act_grad, norm_grads, unit_grads = pl.pallas_call(
        write_kernel,
        out_shape=(
            jax.ShapeDtypeStruct((blocks, tiles, own, width), BF16),
            jax.ShapeDtypeStruct((6, width), F32),
            jax.ShapeDtypeStruct((cores * units,), F32),
        ),
        in_specs=[vmem] * 3,
        out_specs=(hbm,) * 3,
        scratch_shapes=[pltpu.VMEM((cores * units,), F32), dma((tiles + 2,))],
        compiler_params=pltpu.CompilerParams(vmem_limit_bytes=4 * 1024 * 1024),
        name="write",
    )(act, norms, unit_sums)
    act_grad = act_grad.reshape(slots, own, width).transpose(1, 0, 2)
    return (act_grad[None], norm_grads, unit_grads)


def solution(mesh):
    in_specs = (
        P("dp", "enc", "seq", None),
        P("dp", None, None),
        P("dp", None, None),
        P("dp", None, None),
        P("dp", None, "seq", None),
        P("dp", "enc", "seq", None),
        P(),
        P(),
        P(None, "enc"),
        P("enc"),
        P("enc", None),
        P(),
        P(),
        P(),
    )
    out_specs = (P("dp", "enc", "seq", None), P(), P())
    return jax.shard_map(body, mesh=mesh, in_specs=in_specs, out_specs=out_specs, check_vma=False)
```
